256 devices in a mesh: grp: 16 (over y_hi, x, core), dev: 16 (over z, y_lo).
Axes of the slice: x: 4, y: 4 (y_hi: 2, y_lo: 2; y = y_hi * 2 + y_lo), z: 8, core: 2. Of those that a mesh axis runs over, the one named last changes fastest.
Arguments:
- start: float32 [67108864], P(('grp', 'dev')), may hold values from -18 to 18
- hopping: float32 [5, 256, 256], replicated, may hold values from -0.2 to 1.2
- blocks: float32 [5, 256, 256], replicated, may hold values from -0.2 to 1.2
Outputs:
- basis_next: float32 [2, 67108864], P(None, ('grp', 'dev'))
- hessenberg: float32 [5], replicated
The draws below stay inside these ranges and needn't reach their ends.
All inputs are finite; a program needn't handle non-finite values.
Results may differ from the reference program's by a relative error of at most 0.00013.
Values sent between devices are 32-bit elements; how exact they have to be, the bound alone decides.
A program may use at most 64 MiB of HBM per device.

```python
import jax
import jax.numpy as jnp
from jax import lax

SITES = 26
WINDOW = 8
NWIN = 5
STATES = 67108864


def draw_start(key, part):
    ramp = jnp.power(3.0, jnp.arange(STATES, dtype=jnp.float32) / STATES)
    base = jnp.clip(jax.random.normal(key, (STATES,), jnp.float32), -6.0, 6.0)
    return base * ramp


def window_matrix(key, diag_lo, diag_hi, spread):
    order = 2 ** WINDOW
    key_diag, key_noise = jax.random.split(key, 2)
    diag = jax.random.uniform(key_diag, (NWIN, order), jnp.float32, diag_lo, diag_hi)
    noise = jnp.clip(jax.random.normal(key_noise, (NWIN, order, order), jnp.float32), -2.2, 2.2)
    eye = jnp.eye(order, dtype=jnp.float32)
    return noise * spread + eye[None, :, :] * diag[:, :, None]


def draw_hopping(key, part):
    return window_matrix(jax.random.fold_in(key, 11), 0.3, 1.0, 0.5 * 2.0 ** (-WINDOW / 2.0))


def draw_blocks(key, part):
    return window_matrix(jax.random.fold_in(key, 23), 1.0, 1.0, 0.4 * 2.0 ** (-WINDOW / 2.0))


def setup_inputs(seed: int = 0) -> dict:
    streams_of = jax.random.split(jax.random.key(seed), 4)
    return {
        "start": draw_start(jax.random.fold_in(streams_of[3], 71), 0),
        "hopping": draw_hopping(jax.random.fold_in(streams_of[3], 71), 0),
        "blocks": draw_blocks(jax.random.fold_in(streams_of[3], 71), 0),
    }


def window_starts():
    return (0, min(WINDOW - 1, SITES - 8 - WINDOW), SITES - 8 - WINDOW, SITES - 11, SITES - WINDOW)

def window_apply(vector, matrix, first):
    block = vector.reshape(-1, 2 ** WINDOW, 2 ** first)
    return jnp.einsum('pk,bkl->bpl', matrix, block, precision=lax.Precision.HIGHEST).reshape(-1)

def precond_image(vector, hopping, blocks):
    starts = window_starts()
    total = window_apply(vector, hopping[0], starts[0])
    for index in range(1, 5):
        total = total + window_apply(vector, hopping[index], starts[index])
    for index in (4, 3, 2, 1, 0):
        total = window_apply(total, blocks[index], starts[index])
    return total

def arnoldi(basis, vector, hopping, blocks):
    image = precond_image(vector, hopping, blocks)
    coeffs = [jnp.mean(b * image) for b in basis]
    for b, c in zip(basis, coeffs):
        image = image - c * b
    length = jnp.sqrt(jnp.mean(image * image) + 1e-06)
    return (image / length, coeffs, length)

def reference(start, hopping, blocks):
    first = start / jnp.sqrt(jnp.mean(start * start) + 1e-06)
    second, coeffs_one, length_one = arnoldi([first], first, hopping, blocks)
    third, coeffs_two, length_two = arnoldi([first, second], second, hopping, blocks)
    basis_next = jnp.stack([second, third])
    hessenberg = jnp.stack([coeffs_one[0], length_one, coeffs_two[0], coeffs_two[1], length_two])
    return (basis_next, hessenberg)
```

```python
import functools

import jax
import jax.numpy as jnp
from jax import lax
from jax.experimental import pallas as pl
from jax.experimental.pallas import tpu as pltpu
from jax.sharding import PartitionSpec as P

MESH = pl.DeviceIdType.MESH
HI = lax.Precision.HIGHEST
AXES = ("grp", "dev")


def exchange_kernel(ng, nd, x_ref, o_ref, send_sem, recv_sem):
    n = ng * nd
    me = lax.axis_index("grp") * nd + lax.axis_index("dev")
    barrier = pltpu.get_barrier_semaphore()

    def greet(off, carry):
        to = lax.rem(me + off, n)
        pl.semaphore_signal(barrier, inc=1, device_id=(to // nd, to % nd), device_id_type=MESH)
        return carry

    lax.fori_loop(1, n, greet, 0)
    pl.semaphore_wait(barrier, n - 1)

    def send(off, carry):
        to = lax.rem(me + off, n)
        pltpu.make_async_remote_copy(
            src_ref=x_ref.at[to],
            dst_ref=o_ref.at[me],
            send_sem=send_sem,
            recv_sem=recv_sem,
            device_id=(to // nd, to % nd),
            device_id_type=MESH,
        ).start()
        return carry

    lax.fori_loop(1, n, send, 0)
    o_ref[me] = x_ref[me]
    pltpu.make_async_copy(x_ref.at[pl.ds(0, n - 1)], x_ref.at[pl.ds(0, n - 1)], send_sem).wait()
    pltpu.make_async_copy(o_ref.at[pl.ds(0, n - 1)], o_ref.at[pl.ds(0, n - 1)], recv_sem).wait()


def exchange(x, ng, nd):
    vmem = pl.BlockSpec(memory_space=pltpu.VMEM)
    return pl.pallas_call(
        functools.partial(exchange_kernel, ng, nd),
        out_shape=jax.ShapeDtypeStruct(x.shape, x.dtype),
        in_specs=[vmem],
        out_specs=vmem,
        scratch_shapes=[pltpu.SemaphoreType.DMA, pltpu.SemaphoreType.DMA],
        name="exchange",
        compiler_params=pltpu.CompilerParams(collective_id=0, has_side_effects=True),
    )(x)


def per_device(start, hopping, blocks):
    ng, nd = lax.axis_size("grp"), lax.axis_size("dev")
    tiles = ng * nd
    states = float(start.shape[0] * tiles)

    def local(which, mat, v):
        if which == 0:
            u = v.reshape(tiles // 2, 2, 8, 128)
            m = mat.reshape(2, 128, 2, 128)
            return jnp.einsum("apbk,tbsk->tasp", m, u, precision=HI).reshape(v.shape)
        if which in (1, 4):
            return jnp.einsum("pt,tsl->psl", mat, v, precision=HI)
        if which == 2:
            u = v.reshape(32, 8, 8, 128)
            m = mat.reshape(8, 32, 8, 32)
            return jnp.einsum("aphq,qbhl->pbal", m, u, precision=HI).reshape(v.shape)
        u = v.reshape(8, 256, 128)
        return jnp.einsum("pk,bkl->bpl", mat, u, precision=HI).reshape(v.shape)

    def apply(v):
        part = local(0, hopping[0], v) + local(1, hopping[1], v) + local(2, hopping[2], v)
        moved = exchange(v, ng, nd)
        total = exchange(part, ng, nd) + local(3, hopping[3], moved) + local(4, hopping[4], moved)
        total = local(3, blocks[3], local(4, blocks[4], total))
        total = exchange(total, ng, nd)
        for index in (2, 1, 0):
            total = local(index, blocks[index], total)
        return total

    def means(*values):
        return lax.psum(jnp.stack([jnp.sum(v) for v in values]), AXES) / states

    x = start.reshape(8, tiles, 128).transpose(1, 0, 2)
    first = x / jnp.sqrt(means(x * x)[0] + 1e-06)
    image = apply(first)
    h00, square = means(first * image, image * image)
    image = image - h00 * first
    r1 = jnp.sqrt(square - h00 * h00 + 1e-06)
    second = image / r1
    image = apply(second)
    h01, h11, square = means(first * image, second * image, image * image)
    r2 = jnp.sqrt(square - h01 * h01 - h11 * h11 + 1e-06)
    third = (image - h01 * first - h11 * second) / r2
    basis = jnp.stack([second, third]).transpose(0, 2, 1, 3).reshape(2, -1)
    return basis, jnp.stack([h00, r1, h01, h11, r2])


def solution(mesh):
    return jax.shard_map(
        per_device,
        mesh=mesh,
        in_specs=(P(AXES), P(), P()),
        out_specs=(P(None, AXES), P()),
        check_vma=False,
    )
```

```python
import functools

import jax
import jax.numpy as jnp
from jax import lax
from jax.experimental import pallas as pl
from jax.experimental.pallas import tpu as pltpu
from jax.sharding import PartitionSpec as P

MESH = pl.DeviceIdType.MESH
F32 = jnp.float32
BF16 = jnp.bfloat16
AXES = ("grp", "dev")
EPS = 1e-06


def in_two(value):
    high = value.astype(BF16)
    return high, (value - high.astype(F32)).astype(BF16)


def kernel(
    ng, nd, start_hbm, hopping_hbm, blocks_hbm, basis_ref, hess_ref,
    natural, hopping, blocks, mats, x_ref, part, total, image, second, fetched,
    share, shares, load_sem, send_sem, recv_sem, share_send, share_recv,
):
    n = ng * nd
    states = float(n * n * 8 * 128)
    grp, dev = lax.axis_index("grp"), lax.axis_index("dev")
    me = grp * nd + dev
    quarter = n // 4
    barrier = pltpu.get_barrier_semaphore()

    loads = [
        pltpu.make_async_copy(start_hbm, natural, load_sem.at[0]),
        pltpu.make_async_copy(hopping_hbm, hopping, load_sem.at[1]),
        pltpu.make_async_copy(blocks_hbm, blocks, load_sem.at[2]),
    ]
    for load in loads:
        load.start()

    def greet(off, carry):
        to = lax.rem(me + off, n)
        pl.semaphore_signal(barrier, inc=1, device_id=(to // nd, to % nd), device_id_type=MESH)
        return carry

    lax.fori_loop(1, n, greet, 0)


    def send_some(src, which, first):
        dst = fetched.at[which]

        def send(j, carry):
            to = first + lax.rem(me + j, quarter)

            @pl.when(to != me)
            def _():
                pltpu.make_async_remote_copy(
                    src_ref=src.at[pl.ds(pl.multiple_of(to * 8, 8), 8)],
                    dst_ref=dst.at[pl.ds(pl.multiple_of(me * 8, 8), 8)],
                    send_sem=send_sem.at[which],
                    recv_sem=recv_sem.at[which],
                    device_id=(to // nd, to % nd),
                    device_id_type=MESH,
                ).start()

            return carry

        lax.fori_loop(0, quarter, send, 0)

    def keep_own(src, which):
        own = pl.ds(pl.multiple_of(me * 8, 8), 8)
        fetched[which, own, :] = src[own, :]

    def quarter_of(i):
        return lax.rem(me // quarter + i, 4)

    def send_all(src, which):
        def body(i, carry):
            send_some(src, which, quarter_of(i) * quarter)
            return carry

        lax.fori_loop(0, 4, body, 0)
        keep_own(src, which)

    def wait_fetched(which):
        got = fetched.at[which, pl.ds(0, (n - 1) * 8)]
        pltpu.make_async_copy(got, got, recv_sem.at[which]).wait()

    def wait_sent(which):
        got = fetched.at[which, pl.ds(0, (n - 1) * 8)]
        pltpu.make_async_copy(got, got, send_sem.at[which]).wait()


    def prepare(stack, index, slot):
        high, low = in_two(stack[index])
        mats[slot, :, 0:256] = high
        mats[slot, :, 256:512] = low
        mats[slot, :, 512:768] = high

    def times(slot, x):
        high, low = in_two(x)
        return jnp.dot(
            mats[slot], jnp.concatenate([high, high, low], 0), preferred_element_type=F32
        )

    def rows_of(window, b):
        if window in (1, 4):
            return [pl.ds(b, 256, stride=8)]
        if window == 2:
            return [pl.ds(b * 8 + s, 32, stride=64) for s in range(8)]
        return [pl.ds(pl.multiple_of(b * 256, 256), 256)]

    def column_block(window, slot, src, dst, add, i):
        rows = [rows_of(window, 2 * i), rows_of(window, 2 * i + 1)]
        halves = [jnp.concatenate([src[r, :] for r in rs], 0) for rs in rows]
        y = times(slot, jnp.concatenate(halves, 1))
        for h, rs in enumerate(rows):
            size = 256 // len(rs)
            for k, r in enumerate(rs):
                piece = y[k * size : (k + 1) * size, h * 128 : (h + 1) * 128]
                dst[r, :] = dst[r, :] + piece if add else piece

    def row_block(slot, src, dst, add, i):
        rows = pl.ds(pl.multiple_of(i * 512, 512), 512)
        x = src[rows, :].reshape(32, 2, 8, 128)
        x = jnp.concatenate([x[:, 0].reshape(256, 128), x[:, 1].reshape(256, 128)], 1)
        high, low = in_two(x)
        y = lax.dot_general(
            jnp.concatenate([high, high, low], 1),
            mats[slot],
            (((1,), (1,)), ((), ())),
            preferred_element_type=F32,
        )
        y = jnp.stack([y[:, :128].reshape(32, 8, 128), y[:, 128:].reshape(32, 8, 128)], 1)
        y = y.reshape(512, 128)
        dst[rows, :] = dst[rows, :] + y if add else y

    def block(window, slot, src, dst, add, i):
        if window == 0:
            row_block(slot, src, dst, add, i)
        else:
            column_block(window, slot, src, dst, add, i)

    def product(window, slot, src, dst, add=False):
        def body(i, carry):
            block(window, slot, src, dst, add, i)
            return carry

        lax.fori_loop(0, 4, body, 0)

    def product_and_send(window, slot, src, dst, which):
        def body(i, carry):
            q = quarter_of(i)
            block(window, slot, src, dst, False, q)
            send_some(dst, which, q * quarter)
            return carry

        lax.fori_loop(0, 4, body, 0)
        keep_own(dst, which)


    def share_out(k, stage, tile):
        size, at = (nd, dev) if stage == 0 else (ng, grp)
        share[k, stage] = tile
        shares[k, stage, at] = tile
        for off in range(1, size):
            to = lax.rem(at + off, size)
            pltpu.make_async_remote_copy(
                src_ref=share.at[k, stage],
                dst_ref=shares.at[k, stage, at],
                send_sem=share_send.at[k, stage],
                recv_sem=share_recv.at[k, stage],
                device_id=(grp, to) if stage == 0 else (to, dev),
                device_id_type=MESH,
            ).start()

    def gather_in(k, stage):
        size = nd if stage == 0 else ng
        got = shares.at[k, stage, pl.ds(0, size - 1)]
        pltpu.make_async_copy(got, got, share_recv.at[k, stage]).wait()
        pltpu.make_async_copy(got, got, share_send.at[k, stage]).wait()
        return jnp.sum(shares[k, stage, pl.ds(0, size)], 0)

    def means(k):
        tile = jnp.sum(gather_in(k, 1), 1, keepdims=True) / states
        return [tile[i : i + 1] for i in range(3)]

    def partial_sums(terms, count):
        def body(i, carry):
            rows = pl.ds(pl.multiple_of(i * 256, 256), 256)
            return tuple(
                c + jnp.sum(t.reshape(32, 8, 128), 0)
                for c, t in zip(carry, terms(rows), strict=True)
            )

        sums = lax.fori_loop(0, 8, body, (jnp.zeros((8, 128), F32),) * count)
        sums = [jnp.sum(s, 0, keepdims=True) for s in sums]
        return jnp.concatenate(sums + [jnp.zeros((8 - count, 128), F32)], 0)


    loads[0].wait()
    for s in range(8):
        x_ref[pl.ds(s, 256, stride=8), :] = natural[pl.ds(s * 256, 256), :]
    pl.semaphore_wait(barrier, n - 1)
    send_all(x_ref, 0)
    loads[1].wait()
    for index in range(3):
        prepare(hopping, index, index)
    product(1, 1, x_ref, part)
    product(2, 2, x_ref, part, True)
    product(0, 0, x_ref, part, True)
    send_all(part, 1)
    loads[2].wait()
    for index in range(3, 5):
        prepare(hopping, index, index)
    for index in range(5):
        prepare(blocks, index, 5 + index)
    share_out(0, 0, partial_sums(lambda r: (x_ref[r, :] * x_ref[r, :],), 1))

    def upper(which, after_first, after_second):
        wait_fetched(which)
        after_first()
        product(3, 3, fetched.at[which], total)
        product(4, 4, fetched.at[which], total, True)
        wait_fetched(which + 1)

        def add(i, carry):
            rows = pl.ds(pl.multiple_of(i * 256, 256), 256)
            total[rows, :] = total[rows, :] + fetched[which + 1, rows, :]
            return carry

        lax.fori_loop(0, 8, add, 0)
        product(4, 9, total, total)
        product_and_send(3, 8, total, total, which + 2)
        after_second()

    upper(0, lambda: None, lambda: share_out(0, 1, gather_in(0, 0)))
    wait_fetched(2)
    product(2, 7, fetched.at[2], image)
    product(1, 6, image, image)
    wait_sent(1)
    product_and_send(0, 5, image, image, 3)


    product(1, 1, image, part)
    product(2, 2, image, part, True)
    product(0, 0, image, part, True)
    mean_square = means(0)[0]
    scale = 1.0 / jnp.sqrt(mean_square + EPS)

    def first_terms(r):
        return ((x_ref[r, :] * scale) * (image[r, :] * scale),)

    share_out(1, 0, partial_sums(first_terms, 1))
    send_all(part, 4)
    wait_sent(2)
    known = []

    def take_h00():
        h00 = means(1)[0]
        known.append(h00)

        def second_terms(r):
            first = x_ref[r, :] * scale
            left = image[r, :] * scale - h00 * first
            second[r, :] = left
            return (left * left, first * left)

        share_out(2, 0, partial_sums(second_terms, 2))

    upper(3, lambda: share_out(1, 1, gather_in(1, 0)), take_h00)
    h00 = known[0]
    after = natural
    wait_fetched(5)
    product(2, 7, fetched.at[5], after)
    share_out(2, 1, gather_in(2, 0))
    product(1, 6, after, after)
    product(0, 5, after, after)
    left_square, left_first, _ = means(2)
    r1 = jnp.sqrt(left_square + EPS)
    over_r1 = 1.0 / r1

    def third_terms(r):
        moved = (after[r, :] * scale - h00 * (image[r, :] * scale)) * over_r1
        after[r, :] = moved
        return (x_ref[r, :] * scale * moved, second[r, :] * over_r1 * moved, moved * moved)

    share_out(3, 0, partial_sums(third_terms, 3))
    for s in range(8):
        rows = pl.ds(s, 256, stride=8)
        basis_ref[pl.ds(s * 512, 256, stride=2), :] = second[rows, :] * over_r1
    share_out(3, 1, gather_in(3, 0))
    h01, h11, square = means(3)
    gram00 = mean_square * scale * scale
    gram01 = left_first * over_r1
    gram11 = left_square * over_r1 * over_r1
    square = square - 2.0 * (h01 * h01 + h11 * h11)
    square = square + h01 * h01 * gram00 + 2.0 * h01 * h11 * gram01 + h11 * h11 * gram11
    r2 = jnp.sqrt(jnp.maximum(square, 0.0) + EPS)
    over_r2 = 1.0 / r2
    for s in range(8):
        rows = pl.ds(s, 256, stride=8)
        third = after[rows, :] - h01 * (x_ref[rows, :] * scale) - h11 * (second[rows, :] * over_r1)
        basis_ref[pl.ds(s * 512 + 1, 256, stride=2), :] = third * over_r2
    at = lax.broadcasted_iota(jnp.int32, (8, 128), 1)
    hess = jnp.zeros((8, 128), F32)
    for i, value in enumerate((h00, r1, h01, h11, r2)):
        hess = jnp.where(at == i, value, hess)
    hess_ref[...] = hess
    for which in (0, 3, 4, 5):
        wait_sent(which)


def per_device(start, hopping, blocks):
    ng, nd = lax.axis_size("grp"), lax.axis_size("dev")
    rows = start.shape[0] // 128
    anywhere = pl.BlockSpec(memory_space=pl.ANY)
    vmem = pl.BlockSpec(memory_space=pltpu.VMEM)
    vector = pltpu.VMEM((rows, 128), F32)
    dma = pltpu.SemaphoreType.DMA
    basis, hess = pl.pallas_call(
        functools.partial(kernel, ng, nd),
        out_shape=(
            jax.ShapeDtypeStruct((2 * rows, 128), F32),
            jax.ShapeDtypeStruct((8, 128), F32),
        ),
        in_specs=[anywhere] * 3,
        out_specs=(vmem, vmem),
        scratch_shapes=[
            vector,
            pltpu.VMEM(hopping.shape, F32),
            pltpu.VMEM(blocks.shape, F32),
            pltpu.VMEM((10, 256, 768), BF16),
            vector,
            vector,
            vector,
            vector,
            vector,
            pltpu.VMEM((6, rows, 128), F32),
            pltpu.VMEM((4, 2, 8, 128), F32),
            pltpu.VMEM((4, 2, 16, 8, 128), F32),
            dma((3,)),
            dma((6,)),
            dma((6,)),
            dma((4, 2)),
            dma((4, 2)),
        ],
        name="arnoldi",
        compiler_params=pltpu.CompilerParams(
            collective_id=0, has_side_effects=True, vmem_limit_bytes=56 << 20
        ),
    )(start.reshape(rows, 128), hopping, blocks)
    basis = basis.reshape(rows, 2, 128).transpose(1, 0, 2).reshape(2, -1)
    return basis, hess[0, :5]


def solution(mesh):
    return jax.shard_map(
        per_device,
        mesh=mesh,
        in_specs=(P(AXES), P(), P()),
        out_specs=(P(None, AXES), P()),
        check_vma=False,
    )
```

```python
import functools

import jax
import jax.numpy as jnp
from jax import lax
from jax.experimental import pallas as pl
from jax.experimental.pallas import tpu as pltpu
from jax.sharding import PartitionSpec as P

MESH = pl.DeviceIdType.MESH
F32 = jnp.float32
BF16 = jnp.bfloat16
AXES = ("grp", "dev")
EPS = 1e-06


def in_two(value):
    high = value.astype(BF16)
    return high, (value - high.astype(F32)).astype(BF16)


def kernel(
    ng, nd, start_hbm, hopping_hbm, blocks_hbm, basis_hbm, hess_ref,
    natural, hopping, blocks, mats, both, x_ref, part, total, image, second, fetched,
    share, shares, load_sem, send_sem, recv_sem, share_send, share_recv,
):
    n = ng * nd
    states = float(n * n * 8 * 128)
    grp, dev = lax.axis_index("grp"), lax.axis_index("dev")
    me = grp * nd + dev
    quarter = n // 4
    barrier = pltpu.get_barrier_semaphore()

    loads = [
        pltpu.make_async_copy(start_hbm, natural, load_sem.at[0]),
        pltpu.make_async_copy(hopping_hbm, hopping, load_sem.at[1]),
        pltpu.make_async_copy(blocks_hbm, blocks, load_sem.at[2]),
    ]
    for load in loads:
        load.start()

    def greet(off, carry):
        to = lax.rem(me + off, n)
        pl.semaphore_signal(barrier, inc=1, device_id=(to // nd, to % nd), device_id_type=MESH)
        return carry

    lax.fori_loop(1, n, greet, 0)


    def send_some(src, which, first):
        dst = fetched.at[which]

        def send(j, carry):
            to = first + lax.rem(me + j, quarter)

            @pl.when(to != me)
            def _():
                pltpu.make_async_remote_copy(
                    src_ref=src.at[pl.ds(pl.multiple_of(to * 8, 8), 8)],
                    dst_ref=dst.at[pl.ds(pl.multiple_of(me * 8, 8), 8)],
                    send_sem=send_sem.at[which],
                    recv_sem=recv_sem.at[which],
                    device_id=(to // nd, to % nd),
                    device_id_type=MESH,
                ).start()

            return carry

        lax.fori_loop(0, quarter, send, 0)

    def keep_own(src, which):
        own = pl.ds(pl.multiple_of(me * 8, 8), 8)
        fetched[which, own, :] = src[own, :]

    def quarter_of(i):
        return lax.rem(me // quarter + i, 4)

    def send_all(src, which):
        def body(i, carry):
            send_some(src, which, quarter_of(i) * quarter)
            return carry

        lax.fori_loop(0, 4, body, 0)
        keep_own(src, which)

    def wait_fetched(which):
        got = fetched.at[which, pl.ds(0, (n - 1) * 8)]
        pltpu.make_async_copy(got, got, recv_sem.at[which]).wait()

    def wait_sent(which):
        got = fetched.at[which, pl.ds(0, (n - 1) * 8)]
        pltpu.make_async_copy(got, got, send_sem.at[which]).wait()


    def prepare(stack, index, slot):
        high, low = in_two(stack[index])
        mats[slot, :, 0:256] = high
        mats[slot, :, 256:512] = low
        mats[slot, :, 512:768] = high

    def times(slot, x):
        high, low = in_two(x)
        return jnp.dot(
            mats[slot], jnp.concatenate([high, high, low], 0), preferred_element_type=F32
        )

    def rows_of(window, b):
        if window in (1, 4):
            return [pl.ds(b, 256, stride=8)]
        if window == 2:
            return [pl.ds(b * 8 + s, 32, stride=64) for s in range(8)]
        return [pl.ds(pl.multiple_of(b * 256, 256), 256)]

    def column_block(window, slot, src, dst, add, i, other=None):
        rows = [rows_of(window, 2 * i), rows_of(window, 2 * i + 1)]
        if other is None:
            halves = [jnp.concatenate([src[r, :] for r in rs], 0) for rs in rows]
        else:
            halves = [jnp.concatenate([src[r, :] + other[r, :] for r in rs], 0) for rs in rows]
        y = times(slot, jnp.concatenate(halves, 1))
        for h, rs in enumerate(rows):
            size = 256 // len(rs)
            for k, r in enumerate(rs):
                piece = y[k * size : (k + 1) * size, h * 128 : (h + 1) * 128]
                dst[r, :] = dst[r, :] + piece if add else piece

    def row_block(slot, src, dst, add, i):
        rows = pl.ds(pl.multiple_of(i * 512, 512), 512)
        x = src[rows, :].reshape(32, 2, 8, 128)
        x = jnp.concatenate([x[:, 0].reshape(256, 128), x[:, 1].reshape(256, 128)], 1)
        high, low = in_two(x)
        y = lax.dot_general(
            jnp.concatenate([high, high, low], 1),
            mats[slot],
            (((1,), (1,)), ((), ())),
            preferred_element_type=F32,
        )
        y = jnp.stack([y[:, :128].reshape(32, 8, 128), y[:, 128:].reshape(32, 8, 128)], 1)
        y = y.reshape(512, 128)
        dst[rows, :] = dst[rows, :] + y if add else y

    def block(window, slot, src, dst, add, i, other=None):
        if window == 0:
            row_block(slot, src, dst, add, i)
        else:
            column_block(window, slot, src, dst, add, i, other)

    def product(window, slot, src, dst, add=False, other=None):
        def body(i, carry):
            block(window, slot, src, dst, add, i, other)
            return carry

        lax.fori_loop(0, 4, body, 0, unroll=4)

    def product_and_send(window, slot, src, dst, which):
        def body(i, carry):
            q = quarter_of(i)
            block(window, slot, src, dst, False, q)
            send_some(dst, which, q * quarter)
            return carry

        lax.fori_loop(0, 4, body, 0)
        keep_own(dst, which)


    z, y_low = dev // 2, dev % 2

    def share_out(k, stage, row):
        size, at = (32, grp * 2 + y_low) if stage == 0 else (8, z)
        share[k, stage] = row
        shares[k, stage, at] = row
        for off in range(1, size):
            to = lax.rem(at + off, size)
            pltpu.make_async_remote_copy(
                src_ref=share.at[k, stage],
                dst_ref=shares.at[k, stage, at],
                send_sem=share_send.at[k, stage],
                recv_sem=share_recv.at[k, stage],
                device_id=(to // 2, z * 2 + to % 2) if stage == 0 else (grp, to * 2 + y_low),
                device_id_type=MESH,
            ).start()

    def gather_in(k, stage):
        size = 32 if stage == 0 else 8
        got = shares.at[k, stage, pl.ds(0, size - 1)]
        pltpu.make_async_copy(got, got, share_recv.at[k, stage]).wait()
        pltpu.make_async_copy(got, got, share_send.at[k, stage]).wait()
        return jnp.sum(shares[k, stage, pl.ds(0, size)], 0)

    def means(k):
        row = gather_in(k, 1) / states
        return [row[:, i : i + 1] for i in range(3)]

    def add_terms(carry, terms):
        pairs = zip(carry, terms, strict=True)
        return tuple(c + jnp.sum(t.reshape(-1, 8, 128), 0) for c, t in pairs)

    def as_row(sums):
        at = lax.broadcasted_iota(jnp.int32, (1, 128), 1)
        row = jnp.zeros((1, 128), F32)
        for i, value in enumerate(sums):
            value = jnp.sum(jnp.sum(value, 0, keepdims=True), 1, keepdims=True)
            row = jnp.where(at == i, value, row)
        return row

    def zeros(count):
        return (jnp.zeros((8, 128), F32),) * count

    def partial_sums(terms, count):
        def body(i, carry):
            return add_terms(carry, terms(pl.ds(pl.multiple_of(i * 256, 256), 256)))

        return as_row(lax.fori_loop(0, 8, body, zeros(count)))


    loads[0].wait()
    for s in range(8):
        x_ref[pl.ds(s, 256, stride=8), :] = natural[pl.ds(s * 256, 256), :]
    pl.semaphore_wait(barrier, n - 1)
    send_all(x_ref, 0)
    loads[1].wait()
    for index in range(3):
        prepare(hopping, index, index)
    product(1, 1, x_ref, part)
    product(2, 2, x_ref, part, True)
    product(0, 0, x_ref, part, True)
    send_all(part, 1)
    loads[2].wait()
    for index in range(3, 5):
        prepare(hopping, index, index)
    for index in range(5):
        prepare(blocks, index, 5 + index)
    share_out(0, 0, partial_sums(lambda r: (x_ref[r, :] * x_ref[r, :],), 1))

    def send_part(which, start, stop):
        def body(i, carry):
            send_some(part, which, quarter_of(i) * quarter)
            return carry

        lax.fori_loop(start, stop, body, 0)

    wait_fetched(0)
    product(3, 3, fetched.at[0], total)
    product(4, 4, fetched.at[0], total, True)
    wait_fetched(1)
    product(4, 9, total, total, other=fetched.at[1])
    product_and_send(3, 8, total, total, 2)
    share_out(0, 1, gather_in(0, 0))
    wait_fetched(2)
    product(2, 7, fetched.at[2], image)
    product(1, 6, image, image)
    wait_sent(1)
    product_and_send(0, 5, image, image, 3)


    product(1, 1, image, part)
    product(2, 2, image, part, True)
    product(0, 0, image, part, True)
    mean_square = means(0)[0]
    scale = 1.0 / jnp.sqrt(mean_square + EPS)

    def first_terms(r):
        return ((x_ref[r, :] * scale) * (image[r, :] * scale),)

    share_out(1, 0, partial_sums(first_terms, 1))
    send_part(4, 0, 2)
    wait_sent(2)
    wait_fetched(3)
    share_out(1, 1, gather_in(1, 0))
    send_part(4, 2, 4)
    keep_own(part, 4)
    product(3, 3, fetched.at[3], total)
    product(4, 4, fetched.at[3], total, True)
    h00 = means(1)[0]

    def second_terms(r):
        first = x_ref[r, :] * scale
        left = image[r, :] * scale - h00 * first
        second[r, :] = left
        return (left * left, first * left)

    share_out(2, 0, partial_sums(second_terms, 2))
    wait_fetched(4)
    product(4, 9, total, total, other=fetched.at[4])
    share_out(2, 1, gather_in(2, 0))
    product_and_send(3, 8, total, total, 5)
    left_square, left_first, _ = means(2)
    r1 = jnp.sqrt(left_square + EPS)
    over_r1 = 1.0 / r1
    for s in range(8):
        rows = pl.ds(s, 256, stride=8)
        value = second[rows, :] * over_r1
        second[rows, :] = value
        both[pl.ds(s * 512, 256, stride=2), :] = value

    after = natural
    wait_fetched(5)
    product(2, 7, fetched.at[5], after)
    product(1, 6, after, after)

    def last(i, carry):
        row_block(5, after, after, False, i)
        rows = pl.ds(pl.multiple_of(i * 512, 512), 512)
        moved = (after[rows, :] * scale - h00 * (image[rows, :] * scale)) * over_r1
        after[rows, :] = moved
        return add_terms(
            carry, (x_ref[rows, :] * scale * moved, second[rows, :] * moved, moved * moved)
        )

    share_out(3, 0, as_row(lax.fori_loop(0, 4, last, zeros(3), unroll=2)))
    share_out(3, 1, gather_in(3, 0))
    h01, h11, square = means(3)
    gram00 = mean_square * scale * scale
    gram01 = left_first * over_r1
    gram11 = left_square * over_r1 * over_r1
    square = square - 2.0 * (h01 * h01 + h11 * h11)
    square = square + h01 * h01 * gram00 + 2.0 * h01 * h11 * gram01 + h11 * h11 * gram11
    r2 = jnp.sqrt(jnp.maximum(square, 0.0) + EPS)
    over_r2 = 1.0 / r2
    writes = []
    for s in range(8):
        rows = pl.ds(s, 256, stride=8)
        third = after[rows, :] - h01 * (x_ref[rows, :] * scale) - h11 * second[rows, :]
        both[pl.ds(s * 512 + 1, 256, stride=2), :] = third * over_r2
        done = pl.ds(s * 512, 512)
        writes.append(
            pltpu.make_async_copy(both.at[done], basis_hbm.at[done], load_sem.at[3 + s])
        )
        writes[-1].start()
    for i, value in enumerate((h00, r1, h01, h11, r2)):
        hess_ref[i] = value[0, 0]
    for which in (0, 3, 4, 5):
        wait_sent(which)
    for write in writes:
        write.wait()


def per_device(start, hopping, blocks):
    ng, nd = lax.axis_size("grp"), lax.axis_size("dev")
    rows = start.shape[0] // 128
    anywhere = pl.BlockSpec(memory_space=pl.ANY)
    vector = pltpu.VMEM((rows, 128), F32)
    dma = pltpu.SemaphoreType.DMA
    operands = (start.reshape(rows, 128), hopping, blocks)
    basis, hess = pl.pallas_call(
        functools.partial(kernel, ng, nd),
        out_shape=(
            jax.ShapeDtypeStruct((2 * rows, 128), F32),
            jax.ShapeDtypeStruct((5,), F32),
        ),
        in_specs=[pl.BlockSpec(memory_space=pltpu.HBM)] * 3,
        out_specs=(anywhere, pl.BlockSpec(memory_space=pltpu.SMEM)),
        scratch_shapes=[
            vector,
            pltpu.VMEM(hopping.shape, F32),
            pltpu.VMEM(blocks.shape, F32),
            pltpu.VMEM((10, 256, 768), BF16),
            pltpu.VMEM((2 * rows, 128), F32),
            vector,
            vector,
            vector,
            vector,
            vector,
            pltpu.VMEM((6, rows, 128), F32),
            pltpu.VMEM((4, 2, 1, 128), F32),
            pltpu.VMEM((4, 2, 32, 1, 128), F32),
            dma((11,)),
            dma((6,)),
            dma((6,)),
            dma((4, 2)),
            dma((4, 2)),
        ],
        name="arnoldi",
        compiler_params=pltpu.CompilerParams(
            collective_id=0, has_side_effects=True, vmem_limit_bytes=32 << 20
        ),
    )(*[pltpu.with_memory_space_constraint(a, pltpu.HBM) for a in operands])
    basis = basis.reshape(rows, 2, 128).transpose(1, 0, 2).reshape(2, -1)
    return basis, hess


def solution(mesh):
    return jax.shard_map(
        per_device,
        mesh=mesh,
        in_specs=(P(AXES), P(), P()),
        out_specs=(P(None, AXES), P()),
        check_vma=False,
    )
```

```python
import functools

import jax
import jax.numpy as jnp
from jax import lax
from jax.experimental import pallas as pl
from jax.experimental.pallas import tpu as pltpu
from jax.sharding import PartitionSpec as P

MESH = pl.DeviceIdType.MESH
F32 = jnp.float32
BF16 = jnp.bfloat16
AXES = ("grp", "dev")
EPS = 1e-06


def in_two(value):
    high = value.astype(BF16)
    return high, (value - high.astype(F32)).astype(BF16)


def swapped_halves(tiles):
    far = pltpu.roll(pltpu.roll(tiles, 64, 2), 4, 1)
    sub = lax.broadcasted_iota(jnp.int32, tiles.shape, 1) < 4
    lane = lax.broadcasted_iota(jnp.int32, tiles.shape, 2) < 64
    return jnp.where(sub == lane, tiles, far)


def side_by_side(one, two, upper):
    lane = lax.broadcasted_iota(jnp.int32, one.shape, one.ndim - 1) < 64
    if upper:
        return jnp.where(lane, pltpu.roll(one, 64, one.ndim - 1), two)
    return jnp.where(lane, one, pltpu.roll(two, 64, one.ndim - 1))


def kernel(
    ng, nd, start_hbm, hopping_hbm, blocks_hbm, basis_hbm, hess_ref,
    natural, hopping, blocks, mats, both, x_ref, part, total, image, second, fetched,
    share, shares, load_sem, send_sem, recv_sem, share_send, share_recv,
):
    n = ng * nd
    states = float(n * n * 8 * 128)
    grp, dev = lax.axis_index("grp"), lax.axis_index("dev")
    me = grp * nd + dev
    quarter = n // 4
    barrier = pltpu.get_barrier_semaphore()

    loads = [
        pltpu.make_async_copy(start_hbm, natural, load_sem.at[0]),
        pltpu.make_async_copy(hopping_hbm, hopping, load_sem.at[1]),
        pltpu.make_async_copy(blocks_hbm, blocks, load_sem.at[2]),
    ]
    for load in loads:
        load.start()

    def greet(off, carry):
        to = lax.rem(me + off, n)
        pl.semaphore_signal(barrier, inc=1, device_id=(to // nd, to % nd), device_id_type=MESH)
        return carry

    lax.fori_loop(1, n, greet, 0)


    def send_some(src, which, first, half=None):
        dst = fetched.at[which]
        size = 8 if half is None else 4

        def send(j, carry):
            to = first + lax.rem(me + j, quarter)

            @pl.when(to != me)
            def _():
                there, here = (t * 8 + (half or 0) * 4 for t in (to, me))
                pltpu.make_async_remote_copy(
                    src_ref=src.at[pl.ds(pl.multiple_of(there, size), size)],
                    dst_ref=dst.at[pl.ds(pl.multiple_of(here, size), size)],
                    send_sem=send_sem.at[which, half or 0],
                    recv_sem=recv_sem.at[which, half or 0],
                    device_id=(to // nd, to % nd),
                    device_id_type=MESH,
                ).start()

            return carry

        lax.fori_loop(0, quarter, send, 0)

    def keep_own(src, which):
        own = pl.ds(pl.multiple_of(me * 8, 8), 8)
        fetched[which, own, :] = src[own, :]

    def quarter_of(i):
        return lax.rem(me // quarter + i, 4)

    def send_all(src, which, half=None):
        def body(i, carry):
            send_some(src, which, quarter_of(i) * quarter, half)
            return carry

        lax.fori_loop(0, 4, body, 0)

    def wait_for(sems, which, half=None):
        got = fetched.at[which, pl.ds(0, (n - 1) * (8 if half is None else 4))]
        pltpu.make_async_copy(got, got, sems.at[which, half or 0]).wait()

    def wait_fetched(which, half=None):
        wait_for(recv_sem, which, half)

    def wait_sent(which):
        for half in (None,) if which in (0, 3) else (0, 1):
            wait_for(send_sem, which, half)


    def prepare(stack, index, slot):
        high, low = in_two(stack[index])
        mats[slot, :, 0:256] = high
        mats[slot, :, 256:512] = low
        mats[slot, :, 512:768] = high

    def times(slot, x):
        high, low = in_two(x)
        return jnp.dot(
            mats[slot], jnp.concatenate([high, high, low], 0), preferred_element_type=F32
        )

    def rows_of(window, b):
        if window in (1, 4):
            return [pl.ds(b, 256, stride=8)]
        if window == 2:
            return [pl.ds(b * 8 + s, 32, stride=64) for s in range(8)]
        return [pl.ds(pl.multiple_of(b * 256, 256), 256)]

    def lower_rows(src, b):
        pieces = [None] * 8
        for s in range(4):
            one = src[pl.ds(b * 8 + s, 32, stride=64), :]
            two = src[pl.ds(b * 8 + 4 + s, 32, stride=64), :]
            pieces[s] = side_by_side(one, two, False)
            pieces[4 + s] = side_by_side(one, two, True)
        return jnp.concatenate(pieces, 0)

    def column_block(window, slot, src, dst, add, i, other=None):
        rows = [rows_of(window, 2 * i), rows_of(window, 2 * i + 1)]
        if other == "halves":
            halves = [lower_rows(src, 2 * i), lower_rows(src, 2 * i + 1)]
        elif other is None:
            halves = [jnp.concatenate([src[r, :] for r in rs], 0) for rs in rows]
        else:
            halves = [jnp.concatenate([src[r, :] + other[r, :] for r in rs], 0) for rs in rows]
        y = times(slot, jnp.concatenate(halves, 1))
        for h, rs in enumerate(rows):
            size = 256 // len(rs)
            for k, r in enumerate(rs):
                piece = y[k * size : (k + 1) * size, h * 128 : (h + 1) * 128]
                dst[r, :] = dst[r, :] + piece if add else piece

    def row_block(slot, src, dst, add, i, swap=False):
        rows = pl.ds(pl.multiple_of(i * 512, 512), 512)
        x = src[rows, :].reshape(32, 2, 8, 128)
        x = jnp.concatenate([x[:, 0].reshape(256, 128), x[:, 1].reshape(256, 128)], 1)
        high, low = in_two(x)
        y = lax.dot_general(
            jnp.concatenate([high, high, low], 1),
            mats[slot],
            (((1,), (1,)), ((), ())),
            preferred_element_type=F32,
        )
        y = jnp.stack([y[:, :128].reshape(32, 8, 128), y[:, 128:].reshape(32, 8, 128)], 1)
        y = y.reshape(512, 128)
        y = dst[rows, :] + y if add else y
        dst[rows, :] = swapped_halves(y.reshape(64, 8, 128)).reshape(512, 128) if swap else y

    def block(window, slot, src, dst, add, i, other=None):
        if window == 0:
            row_block(slot, src, dst, add, i, other == "swap")
        else:
            column_block(window, slot, src, dst, add, i, other)

    def product(window, slot, src, dst, add=False, other=None, start=0, stop=4):
        def body(i, carry):
            block(window, slot, src, dst, add, i, other)
            return carry

        lax.fori_loop(start, stop, body, 0, unroll=stop - start)

    def product_and_send(window, slot, src, dst, which):
        def body(i, carry):
            q = quarter_of(i)
            block(window, slot, src, dst, False, q)
            send_some(dst, which, q * quarter)
            return carry

        lax.fori_loop(0, 4, body, 0)
        keep_own(dst, which)

    def swap_total():
        def body(i, carry):
            rows = pl.ds(pl.multiple_of(i * 512, 512), 512)
            tiles = total[rows, :].reshape(64, 8, 128)
            total[rows, :] = swapped_halves(tiles).reshape(512, 128)
            return carry

        lax.fori_loop(0, 4, body, 0)

    def half_total(half, i):
        tiles = total.reshape(n, 8, 128)
        at = [pl.ds(pl.multiple_of((4 * i + j) * 32, 32), 32) for j in range(4)]
        held = [swapped_halves(tiles[t]) for t in at]
        pairs = [side_by_side(held[j], held[j + 1], half == 1).reshape(256, 128) for j in (0, 2)]
        y = times(8, jnp.concatenate(pairs, 1))
        for j in range(4):
            back = y[:, (j // 2) * 128 : (j // 2 + 1) * 128].reshape(32, 8, 128)
            if j % 2 != half:
                back = pltpu.roll(back, 64, 2)
            back = swapped_halves(back)
            tiles[at[j], half * 4 : half * 4 + 4, :] = back[:, half * 4 : half * 4 + 4, :]

    def half_total_and_send(half, which):
        def body(h, carry):
            i = lax.rem(me // (2 * quarter) + h, 2)
            half_total(half, i)
            for k in range(2):
                q = 2 * i + lax.rem(me // quarter + k, 2)
                send_some(total, which, q * quarter, half)
            return carry

        lax.fori_loop(0, 2, body, 0)


    z, y_low = dev // 2, dev % 2

    def share_out(k, stage, row):
        size, at = (32, grp * 2 + y_low) if stage == 0 else (8, z)
        share[k, stage] = row
        shares[k, stage, at] = row
        for off in range(1, size):
            to = lax.rem(at + off, size)
            pltpu.make_async_remote_copy(
                src_ref=share.at[k, stage],
                dst_ref=shares.at[k, stage, at],
                send_sem=share_send.at[k, stage],
                recv_sem=share_recv.at[k, stage],
                device_id=(to // 2, z * 2 + to % 2) if stage == 0 else (grp, to * 2 + y_low),
                device_id_type=MESH,
            ).start()

    def gather_in(k, stage):
        size = 32 if stage == 0 else 8
        got = shares.at[k, stage, pl.ds(0, size - 1)]
        pltpu.make_async_copy(got, got, share_recv.at[k, stage]).wait()
        pltpu.make_async_copy(got, got, share_send.at[k, stage]).wait()
        return jnp.sum(shares[k, stage, pl.ds(0, size)], 0)

    def means(k):
        row = gather_in(k, 1) / states
        return [row[:, i : i + 1] for i in range(3)]

    def add_terms(carry, terms):
        pairs = zip(carry, terms, strict=True)
        return tuple(c + jnp.sum(t.reshape(-1, 8, 128), 0) for c, t in pairs)

    def as_row(sums):
        at = lax.broadcasted_iota(jnp.int32, (1, 128), 1)
        row = jnp.zeros((1, 128), F32)
        for i, value in enumerate(sums):
            value = jnp.sum(jnp.sum(value, 0, keepdims=True), 1, keepdims=True)
            row = jnp.where(at == i, value, row)
        return row

    def zeros(count):
        return (jnp.zeros((8, 128), F32),) * count

    def partial_sums(terms, count):
        def body(i, carry):
            return add_terms(carry, terms(pl.ds(pl.multiple_of(i * 256, 256), 256)))

        return as_row(lax.fori_loop(0, 8, body, zeros(count)))


    loads[0].wait()
    for s in range(8):
        x_ref[pl.ds(s, 256, stride=8), :] = natural[pl.ds(s * 256, 256), :]
    pl.semaphore_wait(barrier, n - 1)
    send_all(x_ref, 0)
    keep_own(x_ref, 0)
    loads[1].wait()
    for index in range(3):
        prepare(hopping, index, index)
    product(1, 1, x_ref, part)
    product(2, 2, x_ref, part, True)
    product(0, 0, x_ref, part, True, other="swap")
    send_all(part, 1, 0)
    send_all(part, 1, 1)
    keep_own(part, 1)
    loads[2].wait()
    for index in range(3, 5):
        prepare(hopping, index, index)
    for index in range(5):
        prepare(blocks, index, 5 + index)
    share_out(0, 0, partial_sums(lambda r: (x_ref[r, :] * x_ref[r, :],), 1))

    wait_fetched(0)
    product(3, 3, fetched.at[0], total)
    product(4, 4, fetched.at[0], total, True)
    swap_total()
    for half in range(2):
        wait_fetched(1, half)
        product(4, 9, total, total, False, fetched.at[1], 2 * half, 2 * half + 2)
        half_total_and_send(half, 2)
    keep_own(total, 2)
    share_out(0, 1, gather_in(0, 0))
    wait_fetched(2, 0)
    wait_fetched(2, 1)
    product(2, 7, fetched.at[2], image, other="halves")
    product(1, 6, image, image)
    wait_sent(1)
    product_and_send(0, 5, image, image, 3)


    product(1, 1, image, part)
    product(2, 2, image, part, True)
    product(0, 0, image, part, True, other="swap")
    mean_square = means(0)[0]
    scale = 1.0 / jnp.sqrt(mean_square + EPS)

    def first_terms(r):
        return ((x_ref[r, :] * scale) * (image[r, :] * scale),)

    share_out(1, 0, partial_sums(first_terms, 1))
    send_all(part, 4, 0)
    wait_sent(2)
    wait_fetched(3)
    share_out(1, 1, gather_in(1, 0))
    send_all(part, 4, 1)
    keep_own(part, 4)
    product(3, 3, fetched.at[3], total)
    product(4, 4, fetched.at[3], total, True)
    swap_total()
    h00 = means(1)[0]

    def second_terms(r):
        first = x_ref[r, :] * scale
        left = image[r, :] * scale - h00 * first
        second[r, :] = left
        return (left * left, first * left)

    share_out(2, 0, partial_sums(second_terms, 2))
    for half in range(2):
        wait_fetched(4, half)
        product(4, 9, total, total, False, fetched.at[4], 2 * half, 2 * half + 2)
        if half == 1:
            share_out(2, 1, gather_in(2, 0))
        half_total_and_send(half, 5)
    keep_own(total, 5)
    left_square, left_first, _ = means(2)
    r1 = jnp.sqrt(left_square + EPS)
    over_r1 = 1.0 / r1
    for s in range(8):
        rows = pl.ds(s, 256, stride=8)
        value = second[rows, :] * over_r1
        second[rows, :] = value
        both[pl.ds(s * 512, 256, stride=2), :] = value

    after = natural
    wait_fetched(5, 0)
    wait_fetched(5, 1)
    product(2, 7, fetched.at[5], after, other="halves")
    product(1, 6, after, after)

    def last(i, carry):
        row_block(5, after, after, False, i)
        rows = pl.ds(pl.multiple_of(i * 512, 512), 512)
        moved = (after[rows, :] * scale - h00 * (image[rows, :] * scale)) * over_r1
        after[rows, :] = moved
        return add_terms(
            carry, (x_ref[rows, :] * scale * moved, second[rows, :] * moved, moved * moved)
        )

    share_out(3, 0, as_row(lax.fori_loop(0, 4, last, zeros(3), unroll=2)))
    share_out(3, 1, gather_in(3, 0))
    h01, h11, square = means(3)
    gram00 = mean_square * scale * scale
    gram01 = left_first * over_r1
    gram11 = left_square * over_r1 * over_r1
    square = square - 2.0 * (h01 * h01 + h11 * h11)
    square = square + h01 * h01 * gram00 + 2.0 * h01 * h11 * gram01 + h11 * h11 * gram11
    r2 = jnp.sqrt(jnp.maximum(square, 0.0) + EPS)
    over_r2 = 1.0 / r2
    writes = []
    for s in range(8):
        rows = pl.ds(s, 256, stride=8)
        third = after[rows, :] - h01 * (x_ref[rows, :] * scale) - h11 * second[rows, :]
        both[pl.ds(s * 512 + 1, 256, stride=2), :] = third * over_r2
        done = pl.ds(s * 512, 512)
        writes.append(
            pltpu.make_async_copy(both.at[done], basis_hbm.at[done], load_sem.at[3 + s])
        )
        writes[-1].start()
    for i, value in enumerate((h00, r1, h01, h11, r2)):
        hess_ref[i] = value[0, 0]
    for which in (0, 3, 4, 5):
        wait_sent(which)
    for write in writes:
        write.wait()


def per_device(start, hopping, blocks):
    ng, nd = lax.axis_size("grp"), lax.axis_size("dev")
    rows = start.shape[0] // 128
    anywhere = pl.BlockSpec(memory_space=pl.ANY)
    vector = pltpu.VMEM((rows, 128), F32)
    dma = pltpu.SemaphoreType.DMA
    operands = (start.reshape(rows, 128), hopping, blocks)
    basis, hess = pl.pallas_call(
        functools.partial(kernel, ng, nd),
        out_shape=(
            jax.ShapeDtypeStruct((2 * rows, 128), F32),
            jax.ShapeDtypeStruct((5,), F32),
        ),
        in_specs=[pl.BlockSpec(memory_space=pltpu.HBM)] * 3,
        out_specs=(anywhere, pl.BlockSpec(memory_space=pltpu.SMEM)),
        scratch_shapes=[
            vector,
            pltpu.VMEM(hopping.shape, F32),
            pltpu.VMEM(blocks.shape, F32),
            pltpu.VMEM((10, 256, 768), BF16),
            pltpu.VMEM((2 * rows, 128), F32),
            vector,
            vector,
            vector,
            vector,
            vector,
            pltpu.VMEM((6, rows, 128), F32),
            pltpu.VMEM((4, 2, 1, 128), F32),
            pltpu.VMEM((4, 2, 32, 1, 128), F32),
            dma((11,)),
            dma((6, 2)),
            dma((6, 2)),
            dma((4, 2)),
            dma((4, 2)),
        ],
        name="arnoldi",
        compiler_params=pltpu.CompilerParams(
            collective_id=0, has_side_effects=True, vmem_limit_bytes=32 << 20
        ),
    )(*[pltpu.with_memory_space_constraint(a, pltpu.HBM) for a in operands])
    basis = basis.reshape(rows, 2, 128).transpose(1, 0, 2).reshape(2, -1)
    return basis, hess


def solution(mesh):
    return jax.shard_map(
        per_device,
        mesh=mesh,
        in_specs=(P(AXES), P(), P()),
        out_specs=(P(None, AXES), P()),
        check_vma=False,
    )
```
